32 devices in a mesh: section: 16 (over z, x, core), tensor: 2 (over y).
Axes of the slice: x: 2, y: 2, z: 4, core: 2. Of those that a mesh axis runs over, the one named last changes fastest.
Arguments:
- stream: float32 [16, 512, 8192], P('section', None, 'tensor'), may hold values from -40 to 40
- down_factor: bfloat16 [2, 16, 8192, 512], P(None, 'section', 'tensor'), may hold values from -0.0625 to 0.0625
- router: bfloat16 [2, 16, 8192, 512], P(None, 'section', 'tensor'), may hold values from -0.0625 to 0.0625
- expert_factor: bfloat16 [2, 16, 512, 32], P(None, 'section'), may hold values from -0.25 to 0.25
- core_tensor: bfloat16 [2, 16, 512, 32, 512], P(None, 'section', 'tensor'), may hold values from -0.046875 to 0.046875
- up_factor: bfloat16 [2, 16, 512, 8192], P(None, 'section', None, 'tensor'), may hold values from -0.25 to 0.25
Outputs:
- stream_out: float32 [16, 512, 8192], P('section', None, 'tensor')
The draws below stay inside these ranges and needn't reach their ends.
All inputs are finite; a program needn't handle non-finite values.
Results may differ from the reference program's by a relative error of at most 0.0095.
Values may be sent and summed in bfloat16 or wider, within the bound.
No kernel may reach another device: no remote copies, remote signals or barrier semaphores. Data moves between devices by JAX's collectives and lax.ppermute only.
A program may use at most 192 MiB of HBM per device.

```python
import math
import jax
import jax.numpy as jnp
from jax import lax

D = 8192
EXPERTS = 512
RE = 32
RD = 512
RF = 512
LAPS = 2
TICKS = 6
MB = 512
SECTIONS = 16
FRONT = 8


def draw_stream(key, part):
    subkeys = jax.random.split(key, 3)
    positions = jnp.arange(D, dtype=jnp.float32) / D
    entries = jax.random.normal(subkeys[0], (SECTIONS, MB, D), jnp.float32)
    ramp_up = 1.0 + 5.0 * positions
    row_scale = jnp.exp(jax.random.uniform(subkeys[2], (SECTIONS, MB, 1), jnp.float32, math.log(0.3), math.log(3.0)))
    col_scale = jnp.exp(jax.random.uniform(subkeys[1], (D,), jnp.float32, 0.0, math.log(10.0))) * jnp.sqrt(ramp_up) / 8.0
    return jnp.clip(entries * col_scale * row_scale, -40.0, 40.0).astype(jnp.float32)


def level_of(key, shape, shards, least, high):
    level, own = 1.0, jax.random.fold_in(key, 6)
    for axis_at, blocks in shards:
        heights = jnp.exp(jax.random.uniform(jax.random.fold_in(own, axis_at), (blocks,), jnp.float32, least / len(shards), high / len(shards)))
        level = level * jnp.repeat(heights, shape[axis_at] // blocks).reshape([-1 if axis == axis_at else 1 for axis in range(len(shape))])
    return level


def scatter_about(key, extent, width, limit, cuts=(), kind=jnp.bfloat16):
    values = width * jax.random.normal(key, extent, jnp.float32)
    if cuts:
        values = values * level_of(key, extent, cuts, -0.22, 0.18)
    return jnp.clip(values, -limit, limit).astype(kind)


def setup_inputs(seed: int = 0) -> dict:
    splits = jax.random.split(jax.random.key(seed), 7)
    stream = draw_stream(jax.random.fold_in(splits[6], 71), 0)
    down_factor = scatter_about(splits[1], (LAPS, SECTIONS, D, RD), D ** -0.5, 0.0625, ((1, 16), (2, 2)))
    router = scatter_about(splits[2], (LAPS, SECTIONS, D, EXPERTS), D ** -0.5, 0.0625, ((1, 16), (2, 2)))
    expert_factor = scatter_about(splits[3], (LAPS, SECTIONS, EXPERTS, RE), EXPERTS ** -0.5, 0.25, ((1, 16),))
    core_tensor = scatter_about(splits[4], (LAPS, SECTIONS, RF, RE, RD), (RE * RD) ** -0.5, 0.046875, ((1, 16), (2, 2)))
    up_factor = scatter_about(splits[5], (LAPS, SECTIONS, RF, D), RF ** -0.5, 0.25, ((1, 16), (3, 2)))
    return {"stream": stream, "down_factor": down_factor, "router": router, "expert_factor": expert_factor, "core_tensor": core_tensor, "up_factor": up_factor}


EPSILON = 1e-05

def section_layer(current, down_part, router_part, expert_part, core_part, up_part):
    lowered = current.astype(jnp.bfloat16)
    projected = jnp.dot(lowered, down_part, preferred_element_type=jnp.float32)
    logits = jnp.dot(lowered, router_part, preferred_element_type=jnp.float32)
    factor = lax.rsqrt(lax.optimization_barrier(jnp.sum(current * current, axis=1, keepdims=True)) / D + EPSILON)
    reduced = (projected * factor).astype(jnp.bfloat16)
    gating = jax.nn.sigmoid(logits * factor).astype(jnp.bfloat16)
    mixing = jnp.dot(gating, expert_part, preferred_element_type=jnp.float32).astype(jnp.bfloat16)
    flattened = core_part.reshape(RF * RE, RD)
    partial_value = lax.dot_general(reduced, flattened, (((1,), (1,)), ((), ())), preferred_element_type=jnp.float32)
    partial_value = partial_value.reshape(MB, RF, RE)
    ranked = lax.optimization_barrier(jnp.sum(partial_value * mixing.astype(jnp.float32)[:, None, :], axis=2)).astype(jnp.bfloat16)
    return current + jnp.dot(ranked, up_part, preferred_element_type=jnp.float32)

def reference(stream, down_factor, router, expert_factor, core_tensor, up_factor):
    section_ids = jnp.arange(SECTIONS, dtype=jnp.int32)
    carried = stream
    for tick_index in range(TICKS):
        anchor = (section_ids - tick_index) % SECTIONS
        lap_ids = (anchor < FRONT).astype(jnp.int32) + (section_ids < tick_index).astype(jnp.int32)

        def one_section(section_inputs):
            current, lap_id, section_id = section_inputs
            return section_layer(current, down_factor[lap_id, section_id], router[lap_id, section_id], expert_factor[lap_id, section_id], core_tensor[lap_id, section_id], up_factor[lap_id, section_id])
        advanced = lax.map(one_section, (carried, lap_ids, section_ids))
        carried = jnp.roll(advanced, 1, axis=0)
    return carried
```

```python
import functools

import jax
import jax.numpy as jnp
from jax import lax
from jax.experimental import pallas as pl
from jax.experimental.pallas import tpu as pltpu
from jax.sharding import PartitionSpec as P

TICKS = 6
CHUNKS = 2
EPSILON = 1e-05


def from_behind(value, axis, steps):
    count = lax.axis_size(axis)
    pairs = [(source, (source + steps) % count) for source in range(count)]
    return lax.ppermute(value, axis, pairs)


def largest_divisor(extent, limit):
    size = min(extent, limit)
    while extent % size:
        size -= 1
    return size


def project_body(d_tiles, table, h_ref, down_ref, router_ref, own_ref, sent_ref, square_ref, low_ref):
    step = pl.program_id(0)

    @pl.when(step == 0)
    def _():
        rows, features = low_ref.shape
        partial = jnp.zeros((rows, 128), jnp.float32)
        for at in range(0, features, 128):
            piece = h_ref[:, at : at + 128]
            wide = piece.astype(jnp.float32)
            partial = partial + wide * wide
            low_ref[:, at : at + 128] = piece.astype(jnp.bfloat16)
        square_ref[...] = jnp.sum(partial.T, axis=0, keepdims=True)

    def emit(weight):
        value = jnp.dot(low_ref[...], weight, preferred_element_type=jnp.float32)
        own_ref[...] = value
        sent_ref[...] = value.astype(jnp.bfloat16)

    @pl.when(step < d_tiles)
    def _():
        emit(down_ref[...])

    @pl.when(step >= d_tiles)
    def _():
        emit(router_ref[...])


def project(table, tick, h, row_block, rows, down, router):
    features, d_rank = down.shape[2:]
    experts = router.shape[3]
    block = largest_divisor(d_rank, 256)
    d_tiles, r_tiles = d_rank // block, experts // block
    total = d_rank + experts
    return pl.pallas_call(
        functools.partial(project_body, d_tiles),
        grid_spec=pltpu.PrefetchScalarGridSpec(
            num_scalar_prefetch=1,
            grid=(d_tiles + r_tiles,),
            in_specs=[
                pl.BlockSpec((rows, features), lambda i, t: (row_block, 0), pipeline_mode=pl.Buffered(1)),
                pl.BlockSpec((None, None, features, block), lambda i, t: (t[tick], 0, 0, jnp.minimum(i, d_tiles - 1))),
                pl.BlockSpec((None, None, features, block), lambda i, t: (t[tick], 0, 0, jnp.maximum(i - d_tiles, 0))),
            ],
            out_specs=[
                pl.BlockSpec((rows, block), lambda i, t: (0, i)),
                pl.BlockSpec((rows, block), lambda i, t: (0, i)),
                pl.BlockSpec((1, rows), lambda i, t: (0, 0)),
            ],
            scratch_shapes=[pltpu.VMEM((rows, features), jnp.bfloat16)],
        ),
        out_shape=[
            jax.ShapeDtypeStruct((rows, total), jnp.float32),
            jax.ShapeDtypeStruct((rows, total), jnp.bfloat16),
            jax.ShapeDtypeStruct((1, rows), jnp.float32),
        ],
        cost_estimate=pl.CostEstimate(
            flops=2 * rows * features * total,
            bytes_accessed=2 * features * total + 2 * rows * features + 6 * rows * total,
            transcendentals=0,
        ),
        name="project",
    )(table, h, down, router)


def core_body(others, width, d_rank, table, own_ref, square_ref, *rest):
    sent_refs, squares = rest[:others], rest[others : 2 * others]
    expert_ref, core_ref, out_ref, reduced_ref, mixing_ref, ranked_ref = rest[2 * others :]
    step = pl.program_id(0)

    @pl.when(step == 0)
    def _():
        square = square_ref[...]
        for other in squares:
            square = square + other[...]
        rows = square.shape[1]
        factor = lax.rsqrt(square / width + EPSILON)
        factor = jnp.broadcast_to(factor, (128, rows)).T

        def total(at, size):
            value = own_ref[:, at : at + size]
            for other in sent_refs:
                value = value + other[:, at : at + size].astype(jnp.float32)
            return value

        for at in range(0, d_rank, 128):
            reduced_ref[at : at + 128, :] = (total(at, 128) * factor).astype(jnp.bfloat16).T
        mixing = jnp.zeros(mixing_ref.shape, jnp.float32)
        for at in range(0, expert_ref.shape[1], 128):
            gating = jax.nn.sigmoid(total(d_rank + at, 128) * factor).astype(jnp.bfloat16)
            mixing = mixing + lax.dot_general(
                expert_ref[:, at : at + 128], gating, (((1,), (1,)), ((), ())), preferred_element_type=jnp.float32
            )
        mixing_ref[...] = mixing.astype(jnp.bfloat16).astype(jnp.float32)

    block, ranks, depth = core_ref.shape
    group = 8
    mixing = mixing_ref[...]
    reduced = reduced_ref[...]
    for at in range(0, block, group):
        part = core_ref[at : at + group].reshape(group * ranks, depth)
        value = jnp.dot(part, reduced, preferred_element_type=jnp.float32)
        value = value.reshape(group, ranks, value.shape[1]) * mixing[None]
        ranked_ref[pl.ds(pl.multiple_of(step * block, group) + at, group), :] = jnp.sum(value, axis=1)

    @pl.when(step == pl.num_programs(0) - 1)
    def _():
        out_ref[...] = ranked_ref[...].T.astype(jnp.bfloat16)


def core(table, tick, own, square, sent, squares, expert, core_tensor, width):
    rows, total = own.shape
    ranks, experts = expert.shape[2:]
    f_rank, _, d_rank = core_tensor.shape[2:]
    block = largest_divisor(f_rank, 32)
    others = len(sent)
    whole = lambda i, t: (0, 0)
    return pl.pallas_call(
        functools.partial(core_body, others, width, d_rank),
        grid_spec=pltpu.PrefetchScalarGridSpec(
            num_scalar_prefetch=1,
            grid=(f_rank // block,),
            in_specs=[pl.BlockSpec((rows, total), whole), pl.BlockSpec((1, rows), whole)]
            + [pl.BlockSpec((rows, total), whole)] * others
            + [pl.BlockSpec((1, rows), whole)] * others
            + [
                pl.BlockSpec((None, None, ranks, experts), lambda i, t: (t[tick], 0, 0, 0)),
                pl.BlockSpec((None, None, block, ranks, d_rank), lambda i, t: (t[tick], 0, i, 0, 0)),
            ],
            out_specs=pl.BlockSpec((rows, f_rank), whole),
            scratch_shapes=[
                pltpu.VMEM((d_rank, rows), jnp.bfloat16),
                pltpu.VMEM((ranks, rows), jnp.float32),
                pltpu.VMEM((f_rank, rows), jnp.float32),
            ],
        ),
        out_shape=jax.ShapeDtypeStruct((rows, f_rank), jnp.bfloat16),
        cost_estimate=pl.CostEstimate(
            flops=2 * rows * f_rank * ranks * d_rank,
            bytes_accessed=2 * f_rank * ranks * d_rank + 6 * rows * total,
            transcendentals=rows * experts,
        ),
        name="core",
    )(table, own, square, *sent, *squares, expert, core_tensor)


def advance_body(pieces, table, h_ref, *rest):
    ranked, ups, out_ref = rest[:pieces], rest[pieces : 2 * pieces], rest[2 * pieces]
    value = h_ref[...].astype(jnp.float32)
    for left, right in zip(ranked, ups):
        value = value + jnp.dot(left[...], right[...], preferred_element_type=jnp.float32)
    out_ref[...] = value.astype(out_ref.dtype)


def advance(table, tick, h, row_block, ranked, up):
    pieces = len(ranked)
    rows, f_rank = ranked[0].shape
    features = up.shape[3]
    block = largest_divisor(features, 1024)

    def up_map(shift):
        def index(i, t):
            return (t[tick], 0, lax.rem(t[TICKS] + pieces - shift, pieces), i)

        return index

    return pl.pallas_call(
        functools.partial(advance_body, pieces),
        grid_spec=pltpu.PrefetchScalarGridSpec(
            num_scalar_prefetch=1,
            grid=(features // block,),
            in_specs=[pl.BlockSpec((rows, block), lambda i, t: (row_block, i))]
            + [pl.BlockSpec((rows, f_rank), lambda i, t: (0, 0))] * pieces
            + [pl.BlockSpec((None, None, f_rank, block), up_map(shift)) for shift in range(pieces)],
            out_specs=pl.BlockSpec((rows, block), lambda i, t: (0, i)),
        ),
        out_shape=jax.ShapeDtypeStruct((rows, features), jnp.bfloat16),
        cost_estimate=pl.CostEstimate(
            flops=2 * rows * f_rank * pieces * features,
            bytes_accessed=2 * f_rank * pieces * features + 4 * rows * features,
            transcendentals=0,
        ),
        name="advance",
    )(table, h, *ranked, *([up] * pieces))


def per_device(stream, down_factor, router, expert_factor, core_tensor, up_factor):
    section_id = lax.axis_index("section")
    sections = lax.axis_size("section")
    parts = lax.axis_size("tensor")
    front_edge = sections // 2
    ticks = jnp.arange(TICKS + 1, dtype=jnp.int32)
    laps = ((section_id - ticks) % sections < front_edge).astype(jnp.int32) + (section_id < ticks).astype(jnp.int32)
    table = jnp.where(ticks < TICKS, laps, lax.axis_index("tensor"))
    expert = jnp.swapaxes(expert_factor, 2, 3)
    width = stream.shape[2] * parts
    rows = stream.shape[1] // CHUNKS
    held = [(stream[0], at) for at in range(CHUNKS)]
    for tick in range(TICKS):
        projected = [project(table, tick, h, at, rows, down_factor, router) for h, at in held]
        if parts > 2:
            projected = [
                (lax.psum(own, "tensor"), sent, lax.psum(square, "tensor")) for own, sent, square in projected
            ]
        arrived = [
            [(from_behind(sent, "tensor", 1), from_behind(square, "tensor", 1))] if parts == 2 else []
            for _, sent, square in projected
        ]
        ranked = [
            core(
                table, tick, own, square, [sent for sent, _ in other], [squares for _, squares in other],
                expert, core_tensor, width,
            )
            for (own, _, square), other in zip(projected, arrived)
        ]
        if parts > 2:
            gathered = [[lax.all_gather(piece, "tensor", axis=1, tiled=True)] for piece in ranked]
        else:
            gathered = [[piece] + [from_behind(piece, "tensor", 1)] * (parts - 1) for piece in ranked]
        advanced = [
            advance(table, tick, h, at, pieces, up_factor) for (h, at), pieces in zip(held, gathered)
        ]
        held = [(from_behind(value, "section", 1), 0) for value in advanced]
    return jnp.concatenate([value for value, _ in held], axis=0).astype(jnp.float32)[None]


def solution(mesh):
    return jax.shard_map(
        per_device,
        mesh=mesh,
        in_specs=(
            P("section", None, "tensor"),
            P(None, "section", "tensor", None),
            P(None, "section", "tensor", None),
            P(None, "section", None, None),
            P(None, "section", "tensor", None, None),
            P(None, "section", None, "tensor"),
        ),
        out_specs=P("section", None, "tensor"),
        check_vma=False,
    )
```

```python
import functools

import jax
import jax.numpy as jnp
from jax import lax
from jax.experimental import pallas as pl
from jax.experimental.pallas import tpu as pltpu
from jax.sharding import PartitionSpec as P


TICKS = 6
CHUNKS = 4
LEAD = 2
PIECES = 4
EPSILON = 1e-05
LANES = 128

IN_VMEM = pl.BlockSpec(memory_space=pltpu.VMEM)
IN_HBM = pl.BlockSpec(memory_space=pltpu.HBM)
IN_SMEM = pl.BlockSpec(memory_space=pltpu.SMEM)
ANYWHERE = pl.BlockSpec(memory_space=pl.ANY)


def from_behind(value, axis, steps):
    count = lax.axis_size(axis)
    pairs = [(source, (source + steps) % count) for source in range(count)]
    return lax.ppermute(value, axis, pairs)


def largest_divisor(extent, limit):
    size = min(extent, limit)
    while extent % size:
        size -= 1
    return size


def params():
    return pltpu.CompilerParams(vmem_limit_bytes=10 << 20)


def fetch_copies(sources, targets, semaphores, places):
    copies = []
    for at, (source, target, place) in enumerate(zip(sources, targets, places)):
        extent = target.shape[0] // PIECES
        for piece in range(PIECES):
            copies.append(
                pltpu.make_async_copy(
                    source.at[(*place[:-1], pl.ds(place[-1] + piece * extent, extent))],
                    target.at[pl.ds(piece * extent, extent)],
                    semaphores.at[at, piece],
                )
            )
    return copies


def fetch_body(count, tick, first, table_ref, stream_ref, *refs):
    sources, h_ref, targets, semaphores = refs[:count], refs[count], refs[count + 1 : -1], refs[-1]
    lap = table_ref[tick]
    copies = fetch_copies(
        (stream_ref, *sources), (h_ref, *targets), semaphores, [(0, first)] + [(lap, 0, 0)] * count
    )
    for copy in copies:
        copy.start()
    for copy in copies:
        copy.wait()


def fetch(table, tick, stream, first, rows, stacked):
    count = len(stacked)
    features = stream.shape[2]
    return pl.pallas_call(
        functools.partial(fetch_body, count, tick, first),
        in_specs=[IN_SMEM] + [IN_HBM] * (1 + count),
        out_specs=[IN_VMEM] * (1 + count),
        out_shape=[pltpu.VMEM((rows, features), stream.dtype)]
        + [pltpu.VMEM(value.shape[2:], value.dtype) for value in stacked],
        scratch_shapes=[pltpu.SemaphoreType.DMA((1 + count, PIECES))],
        compiler_params=params(),
        cost_estimate=pl.CostEstimate(
            flops=0, transcendentals=0, bytes_accessed=sum(value.size * value.dtype.itemsize for value in stacked)
        ),
        name="fetch",
    )(table, stream, *stacked)


def refresh_body(count, tick, table_ref, *refs):
    sources = refs[:count]
    targets, semaphores = refs[-1 - count : -1], refs[-1]

    @pl.when(table_ref[tick] != table_ref[tick - 1])
    def _():
        copies = fetch_copies(sources, targets, semaphores, [(table_ref[tick], 0, 0)] * count)
        for copy in copies:
            copy.start()
        for copy in copies:
            copy.wait()


def refresh(table, tick, stacked, resident, after):
    count = len(stacked)
    return pl.pallas_call(
        functools.partial(refresh_body, count, tick),
        in_specs=[IN_SMEM] + [IN_HBM] * count + [IN_VMEM] * count + [ANYWHERE] * len(after),
        out_specs=[IN_VMEM] * count,
        out_shape=[pltpu.VMEM(value.shape, value.dtype) for value in resident],
        input_output_aliases={1 + count + at: at for at in range(count)},
        scratch_shapes=[pltpu.SemaphoreType.DMA((count, PIECES))],
        compiler_params=params(),
        cost_estimate=pl.CostEstimate(flops=0, transcendentals=0, bytes_accessed=0),
        name="refresh",
    )(table, *stacked, *resident, *after)


def project_body(h_ref, down_ref, router_ref, *rest):
    own_ref, square_ref, sent_ref = rest[-3:]
    rows, features = h_ref.shape
    partial = jnp.zeros((rows, LANES), jnp.float32)
    for at in range(0, features, LANES):
        wide = h_ref[:, at : at + LANES].astype(jnp.float32)
        partial = partial + wide * wide
    square = jnp.broadcast_to(jnp.sum(partial, axis=1, keepdims=True), (rows, LANES))
    square_ref[...] = square
    upper = square.astype(jnp.bfloat16)
    lower = (square - upper.astype(jnp.float32)).astype(jnp.bfloat16)
    lane = lax.broadcasted_iota(jnp.int32, (rows, LANES), 1)
    start = 0
    for weight_ref in (down_ref, router_ref):
        extent = weight_ref.shape[1]
        block = largest_divisor(extent, 256)
        for at in range(0, extent, block):
            value = jnp.dot(
                h_ref[...].astype(jnp.bfloat16), weight_ref[:, at : at + block], preferred_element_type=jnp.float32
            )
            own_ref[:, start + at : start + at + block] = value
            sent_ref[:, start + at : start + at + block] = value.astype(jnp.bfloat16)
        start += extent
    sent_ref[:, start:] = jnp.where(
        lane < LANES // 2, upper.astype(jnp.float32), lower.astype(jnp.float32)
    ).astype(jnp.bfloat16)


def project(h, down, router, after):
    rows, features = h.shape
    total = down.shape[1] + router.shape[1]
    return pl.pallas_call(
        project_body,
        in_specs=[IN_VMEM] * 3 + [ANYWHERE] * len(after),
        out_specs=[IN_VMEM] * 3,
        out_shape=[
            jax.ShapeDtypeStruct((rows, total), jnp.float32),
            jax.ShapeDtypeStruct((rows, LANES), jnp.float32),
            jax.ShapeDtypeStruct((rows, total + LANES), jnp.bfloat16),
        ],
        compiler_params=params(),
        cost_estimate=pl.CostEstimate(
            flops=2 * rows * features * total, bytes_accessed=6 * rows * total, transcendentals=0
        ),
        name="project",
    )(h, down, router, *after)


def core_body(others, width, tick, table_ref, own_ref, square_ref, *rest):
    sent_refs = rest[:others]
    expert_ref, core_ref = rest[others : others + 2]
    out_ref, reduced_ref, mixing_ref, ranked_ref = rest[-4:]
    d_rank, rows = reduced_ref.shape
    experts = expert_ref.shape[2]
    lap = table_ref[tick]
    square = square_ref[...]
    tail = d_rank + experts
    for other in sent_refs:
        pair = other[:, tail:].astype(jnp.float32)
        square = square + pair[:, :1] + pair[:, LANES // 2 : LANES // 2 + 1]
    factor = lax.rsqrt(square / width + EPSILON)

    def total(at):
        value = own_ref[:, at : at + LANES]
        for other in sent_refs:
            value = value + other[:, at : at + LANES].astype(jnp.float32)
        return value

    for at in range(0, d_rank, LANES):
        reduced_ref[at : at + LANES, :] = (total(at) * factor).astype(jnp.bfloat16).T
    mixing = jnp.zeros(mixing_ref.shape, jnp.float32)
    for at in range(0, experts, LANES):
        gating = jax.nn.sigmoid(total(d_rank + at) * factor).astype(jnp.bfloat16)
        mixing = mixing + lax.dot_general(
            expert_ref[lap, :, at : at + LANES],
            gating,
            (((1,), (1,)), ((), ())),
            preferred_element_type=jnp.float32,
        )
    mixing_ref[...] = mixing.astype(jnp.bfloat16).astype(jnp.float32)

    f_rank, ranks, depth = core_ref.shape
    group = largest_divisor(f_rank, 32)
    for at in range(0, f_rank, group):
        part = core_ref[at : at + group].reshape(group * ranks, depth)
        value = jnp.dot(part, reduced_ref[...], preferred_element_type=jnp.float32)
        value = value.reshape(group, ranks, rows) * mixing_ref[...][None]
        ranked_ref[at : at + group, :] = jnp.sum(value, axis=1)
    out_ref[...] = ranked_ref[...].T.astype(jnp.bfloat16)


def core(table, tick, own, square, sent, expert, core_tensor, width, after):
    rows = own.shape[0]
    f_rank, ranks, d_rank = core_tensor.shape
    others = len(sent)
    return pl.pallas_call(
        functools.partial(core_body, others, width, tick),
        in_specs=[IN_SMEM] + [IN_VMEM] * (4 + others) + [ANYWHERE] * len(after),
        out_specs=IN_VMEM,
        out_shape=jax.ShapeDtypeStruct((rows, f_rank), jnp.bfloat16),
        scratch_shapes=[
            pltpu.VMEM((d_rank, rows), jnp.bfloat16),
            pltpu.VMEM((ranks, rows), jnp.float32),
            pltpu.VMEM((f_rank, rows), jnp.float32),
        ],
        compiler_params=params(),
        cost_estimate=pl.CostEstimate(
            flops=2 * rows * f_rank * ranks * d_rank, bytes_accessed=6 * rows * d_rank, transcendentals=rows * d_rank
        ),
        name="core",
    )(table, own, square, *sent, expert, core_tensor, *after)


def advance_body(pieces, table_ref, h_ref, *rest):
    ranked, up_ref, out_ref = rest[:pieces], rest[pieces], rest[-1]
    features = h_ref.shape[1]
    extent = ranked[0].shape[1]
    block = largest_divisor(features, 512)
    for at in range(0, features, block):
        value = h_ref[:, at : at + block].astype(jnp.float32)
        for shift, piece in enumerate(ranked):
            row = pl.multiple_of(lax.rem(table_ref[TICKS] + pieces - shift, pieces) * extent, extent)
            value = value + jnp.dot(
                piece[...], up_ref[pl.ds(row, extent), at : at + block], preferred_element_type=jnp.float32
            )
        out_ref[:, at : at + block] = value.astype(jnp.bfloat16)


def advance(table, h, ranked, up, after):
    pieces = len(ranked)
    rows, features = h.shape
    return pl.pallas_call(
        functools.partial(advance_body, pieces),
        in_specs=[IN_SMEM] + [IN_VMEM] * (2 + pieces) + [ANYWHERE] * len(after),
        out_specs=IN_VMEM,
        out_shape=jax.ShapeDtypeStruct((rows, features), jnp.bfloat16),
        compiler_params=params(),
        cost_estimate=pl.CostEstimate(
            flops=2 * rows * up.shape[0] * features, bytes_accessed=4 * rows * features, transcendentals=0
        ),
        name="advance",
    )(table, h, *ranked, up, *after)


def store_body(first, *refs):
    h_ref, (out_ref, wide_ref, semaphores) = refs[0], refs[-3:]
    rows = h_ref.shape[0]
    extent = rows // PIECES
    copies = []
    for piece in range(PIECES):
        part = pl.ds(piece * extent, extent)
        wide_ref[part, :] = h_ref[part, :].astype(wide_ref.dtype)
        copy = pltpu.make_async_copy(
            wide_ref.at[part], out_ref.at[0, pl.ds(first + piece * extent, extent)], semaphores.at[piece]
        )
        copy.start()
        copies.append(copy)
    for copy in copies:
        copy.wait()


def store(h, first, shape, dtype, out):
    held = [] if out is None else [out]
    return pl.pallas_call(
        functools.partial(store_body, first),
        in_specs=[IN_VMEM] + [ANYWHERE] * len(held),
        out_specs=ANYWHERE,
        out_shape=jax.ShapeDtypeStruct(shape, dtype),
        input_output_aliases={1: 0} if held else {},
        scratch_shapes=[pltpu.VMEM(h.shape, dtype), pltpu.SemaphoreType.DMA((PIECES,))],
        compiler_params=params(),
        cost_estimate=pl.CostEstimate(flops=0, transcendentals=0, bytes_accessed=6 * h.size),
        name="store",
    )(h, *held)


def per_device(stream, down_factor, router, expert_factor, core_tensor, up_factor):
    section_id = lax.axis_index("section")
    sections = lax.axis_size("section")
    parts = lax.axis_size("tensor")
    front_edge = sections // 2
    ticks = jnp.arange(TICKS + 1, dtype=jnp.int32)
    laps = ((section_id - ticks) % sections < front_edge).astype(jnp.int32) + (section_id < ticks).astype(jnp.int32)
    table = jnp.where(ticks < TICKS, laps, lax.axis_index("tensor"))
    expert = jnp.swapaxes(expert_factor[:, 0], 1, 2)
    width = stream.shape[2] * parts
    rows = stream.shape[1] // CHUNKS
    stream, *stacked = [
        pltpu.with_memory_space_constraint(value, pltpu.HBM)
        for value in (stream, down_factor, router, core_tensor, up_factor)
    ]
    held, resident = [], []
    for chunk in range(CHUNKS):
        share = stacked[:2] if chunk == 0 else stacked[2:] if chunk == 1 else []
        h, *fetched = fetch(table, 0, stream, chunk * rows, rows, share)
        held.append(h)
        resident += fetched
    early, late = resident[:2], resident[2:]

    def exchange(own, square, sent):
        if parts == 2:
            return own, square, [from_behind(sent, "tensor", 1)]
        if parts > 2:
            return lax.psum(own, "tensor"), lax.psum(square, "tensor"), []
        return own, square, []

    def gather(piece):
        if parts > 2:
            return [lax.all_gather(piece, "tensor", axis=1, tiled=True)]
        return [piece] + [from_behind(piece, "tensor", 1)] * (parts - 1)

    steps = TICKS * CHUNKS
    projected = [exchange(*project(held[at], *early, [])) for at in range(LEAD)]
    piece = core(table, 0, *projected[0], expert, late[0], width, [])
    for step in range(steps):
        tick, chunk = divmod(step, CHUNKS)
        order = []
        if step + LEAD < steps:
            ahead_tick, ahead = divmod(step + LEAD, CHUNKS)
            own, square, sent = project(held[ahead], *early, [piece])
            order = [sent]
            if ahead == CHUNKS - 1 and ahead_tick + 1 < TICKS:
                early = refresh(table, ahead_tick + 1, stacked[:2], early, order)
                order = order + [early[0]]
            projected.append(exchange(own, square, sent))
        pieces = gather(piece)
        value = advance(table, held[chunk], pieces, late[1], order)
        held[chunk] = from_behind(value, "section", 1)
        if step + 1 < steps:
            if chunk == CHUNKS - 1:
                late = refresh(table, tick + 1, stacked[2:], late, [value])
            piece = core(
                table, (step + 1) // CHUNKS, *projected[step + 1], expert, late[0], width, [value]
            )
    out = None
    for chunk, h in enumerate(held):
        out = store(h, chunk * rows, stream.shape, stream.dtype, out)
    return out


def solution(mesh):
    return jax.shard_map(
        per_device,
        mesh=mesh,
        in_specs=(
            P("section", None, "tensor"),
            P(None, "section", "tensor", None),
            P(None, "section", "tensor", None),
            P(None, "section", None, None),
            P(None, "section", "tensor", None, None),
            P(None, "section", None, "tensor"),
        ),
        out_specs=P("section", None, "tensor"),
        check_vma=False,
    )
```

```python
import functools

import jax
import jax.numpy as jnp
from jax import lax
from jax.experimental import pallas as pl
from jax.experimental.pallas import tpu as pltpu
from jax.sharding import PartitionSpec as P


TICKS = 6
SHARES = (4, 4, 4, 4)
CHUNKS = len(SHARES)
LEAD = 2
PIECES = 4
EPSILON = 1e-05
LANES = 128

IN_VMEM = pl.BlockSpec(memory_space=pltpu.VMEM)
IN_HBM = pl.BlockSpec(memory_space=pltpu.HBM)
IN_SMEM = pl.BlockSpec(memory_space=pltpu.SMEM)
ANYWHERE = pl.BlockSpec(memory_space=pl.ANY)


def from_behind(value, axis, steps):
    count = lax.axis_size(axis)
    pairs = [(source, (source + steps) % count) for source in range(count)]
    return lax.ppermute(value, axis, pairs)


def largest_divisor(extent, limit):
    size = min(extent, limit)
    while extent % size:
        size -= 1
    return size


def params():
    return pltpu.CompilerParams(vmem_limit_bytes=10 << 20)


def fetch_copies(sources, targets, semaphores, places):
    copies = []
    for at, (source, target, place) in enumerate(zip(sources, targets, places)):
        extent = target.shape[0] // PIECES
        for piece in range(PIECES):
            copies.append(
                pltpu.make_async_copy(
                    source.at[(*place[:-1], pl.ds(place[-1] + piece * extent, extent))],
                    target.at[pl.ds(piece * extent, extent)],
                    semaphores.at[at, piece],
                )
            )
    return copies


def fetch_body(count, tick, blocks, table_ref, stream_ref, *refs):
    sources, targets, semaphores = refs[:count], refs[-1 - count - len(blocks) : -1], refs[-1]
    lap = table_ref[tick]
    copies = fetch_copies(
        (*sources, *([stream_ref] * len(blocks))),
        targets,
        semaphores,
        [(lap, 0, 0)] * count + [(0, first) for first, _ in blocks],
    )
    for copy in copies:
        copy.start()
    for copy in copies:
        copy.wait()


def fetch(table, tick, stream, blocks, stacked, after):
    count = len(stacked)
    features = stream.shape[2]
    return pl.pallas_call(
        functools.partial(fetch_body, count, tick, blocks),
        in_specs=[IN_SMEM] + [IN_HBM] * (1 + count) + [ANYWHERE] * len(after),
        out_specs=[IN_VMEM] * (count + len(blocks)),
        out_shape=[pltpu.VMEM(value.shape[2:], value.dtype) for value in stacked]
        + [pltpu.VMEM((rows, features), stream.dtype) for _, rows in blocks],
        scratch_shapes=[pltpu.SemaphoreType.DMA((count + len(blocks), PIECES))],
        compiler_params=params(),
        cost_estimate=pl.CostEstimate(
            flops=0, transcendentals=0, bytes_accessed=sum(value.size * value.dtype.itemsize for value in stacked)
        ),
        name="fetch",
    )(table, stream, *stacked, *after)


def refresh_body(count, tick, table_ref, *refs):
    sources = refs[:count]
    targets, semaphores = refs[-1 - count : -1], refs[-1]

    @pl.when(table_ref[tick] != table_ref[tick - 1])
    def _():
        copies = fetch_copies(sources, targets, semaphores, [(table_ref[tick], 0, 0)] * count)
        for copy in copies:
            copy.start()
        for copy in copies:
            copy.wait()


def refresh(table, tick, stacked, resident, after):
    count = len(stacked)
    return pl.pallas_call(
        functools.partial(refresh_body, count, tick),
        in_specs=[IN_SMEM] + [IN_HBM] * count + [IN_VMEM] * count + [ANYWHERE] * len(after),
        out_specs=[IN_VMEM] * count,
        out_shape=[pltpu.VMEM(value.shape, value.dtype) for value in resident],
        input_output_aliases={1 + count + at: at for at in range(count)},
        scratch_shapes=[pltpu.SemaphoreType.DMA((count, PIECES))],
        compiler_params=params(),
        cost_estimate=pl.CostEstimate(flops=0, transcendentals=0, bytes_accessed=0),
        name="refresh",
    )(table, *stacked, *resident, *after)


def project_body(h_ref, down_ref, router_ref, *rest):
    own_ref, square_ref, sent_ref = rest[-3:]
    rows, features = h_ref.shape
    partial = jnp.zeros((rows, LANES), jnp.float32)
    for at in range(0, features, LANES):
        wide = h_ref[:, at : at + LANES].astype(jnp.float32)
        partial = partial + wide * wide
    square = jnp.broadcast_to(jnp.sum(partial, axis=1, keepdims=True), (rows, LANES))
    square_ref[...] = square
    upper = square.astype(jnp.bfloat16)
    lower = (square - upper.astype(jnp.float32)).astype(jnp.bfloat16)
    lane = lax.broadcasted_iota(jnp.int32, (rows, LANES), 1)
    start = 0
    for weight_ref in (down_ref, router_ref):
        extent = weight_ref.shape[1]
        block = largest_divisor(extent, 256)
        for at in range(0, extent, block):
            value = jnp.dot(
                h_ref[...].astype(jnp.bfloat16), weight_ref[:, at : at + block], preferred_element_type=jnp.float32
            )
            own_ref[:, start + at : start + at + block] = value
            sent_ref[:, start + at : start + at + block] = value.astype(jnp.bfloat16)
        start += extent
    sent_ref[:, start:] = jnp.where(
        lane < LANES // 2, upper.astype(jnp.float32), lower.astype(jnp.float32)
    ).astype(jnp.bfloat16)


def project(h, down, router, after):
    rows, features = h.shape
    total = down.shape[1] + router.shape[1]
    return pl.pallas_call(
        project_body,
        in_specs=[IN_VMEM] * 3 + [ANYWHERE] * len(after),
        out_specs=[IN_VMEM] * 3,
        out_shape=[
            jax.ShapeDtypeStruct((rows, total), jnp.float32),
            jax.ShapeDtypeStruct((rows, LANES), jnp.float32),
            jax.ShapeDtypeStruct((rows, total + LANES), jnp.bfloat16),
        ],
        compiler_params=params(),
        cost_estimate=pl.CostEstimate(
            flops=2 * rows * features * total, bytes_accessed=6 * rows * total, transcendentals=0
        ),
        name="project",
    )(h, down, router, *after)


def core_body(others, width, tick, table_ref, own_ref, square_ref, *rest):
    sent_refs = rest[:others]
    expert_ref, core_ref = rest[others : others + 2]
    out_ref, reduced_ref, mixing_ref, ranked_ref = rest[-4:]
    d_rank, rows = reduced_ref.shape
    experts = expert_ref.shape[2]
    lap = table_ref[tick]
    square = square_ref[...]
    tail = d_rank + experts
    for other in sent_refs:
        pair = other[:, tail:].astype(jnp.float32)
        square = square + pair[:, :1] + pair[:, LANES // 2 : LANES // 2 + 1]
    factor = lax.rsqrt(square / width + EPSILON)

    def total(at):
        value = own_ref[:, at : at + LANES]
        for other in sent_refs:
            value = value + other[:, at : at + LANES].astype(jnp.float32)
        return value

    for at in range(0, d_rank, LANES):
        reduced_ref[at : at + LANES, :] = (total(at) * factor).astype(jnp.bfloat16).T
    mixing = jnp.zeros(mixing_ref.shape, jnp.float32)
    for at in range(0, experts, LANES):
        gating = jax.nn.sigmoid(total(d_rank + at) * factor).astype(jnp.bfloat16)
        mixing = mixing + lax.dot_general(
            expert_ref[lap, :, at : at + LANES],
            gating,
            (((1,), (1,)), ((), ())),
            preferred_element_type=jnp.float32,
        )
    mixing_ref[...] = mixing.astype(jnp.bfloat16).astype(jnp.float32)

    f_rank, ranks, depth = core_ref.shape
    group = largest_divisor(f_rank, 32)
    for at in range(0, f_rank, group):
        part = core_ref[at : at + group].reshape(group * ranks, depth)
        value = jnp.dot(part, reduced_ref[...], preferred_element_type=jnp.float32)
        value = value.reshape(group, ranks, rows) * mixing_ref[...][None]
        ranked_ref[at : at + group, :] = jnp.sum(value, axis=1)
    out_ref[...] = ranked_ref[...].T.astype(jnp.bfloat16)


def core(table, tick, own, square, sent, expert, core_tensor, width, after):
    rows = own.shape[0]
    f_rank, ranks, d_rank = core_tensor.shape
    others = len(sent)
    return pl.pallas_call(
        functools.partial(core_body, others, width, tick),
        in_specs=[IN_SMEM] + [IN_VMEM] * (4 + others) + [ANYWHERE] * len(after),
        out_specs=IN_VMEM,
        out_shape=jax.ShapeDtypeStruct((rows, f_rank), jnp.bfloat16),
        scratch_shapes=[
            pltpu.VMEM((d_rank, rows), jnp.bfloat16),
            pltpu.VMEM((ranks, rows), jnp.float32),
            pltpu.VMEM((f_rank, rows), jnp.float32),
        ],
        compiler_params=params(),
        cost_estimate=pl.CostEstimate(
            flops=2 * rows * f_rank * ranks * d_rank, bytes_accessed=6 * rows * d_rank, transcendentals=rows * d_rank
        ),
        name="core",
    )(table, own, square, *sent, expert, core_tensor, *after)


def advance_body(pieces, table_ref, h_ref, *rest):
    ranked, up_ref, out_ref = rest[:pieces], rest[pieces], rest[-1]
    features = h_ref.shape[1]
    extent = ranked[0].shape[1]
    block = largest_divisor(features, 512)
    for at in range(0, features, block):
        value = h_ref[:, at : at + block].astype(jnp.float32)
        for shift, piece in enumerate(ranked):
            row = pl.multiple_of(lax.rem(table_ref[TICKS] + pieces - shift, pieces) * extent, extent)
            value = value + jnp.dot(
                piece[...], up_ref[pl.ds(row, extent), at : at + block], preferred_element_type=jnp.float32
            )
        out_ref[:, at : at + block] = value.astype(jnp.bfloat16)


def advance(table, h, ranked, up, after):
    pieces = len(ranked)
    rows, features = h.shape
    return pl.pallas_call(
        functools.partial(advance_body, pieces),
        in_specs=[IN_SMEM] + [IN_VMEM] * (2 + pieces) + [ANYWHERE] * len(after),
        out_specs=IN_VMEM,
        out_shape=jax.ShapeDtypeStruct((rows, features), jnp.bfloat16),
        compiler_params=params(),
        cost_estimate=pl.CostEstimate(
            flops=2 * rows * up.shape[0] * features, bytes_accessed=4 * rows * features, transcendentals=0
        ),
        name="advance",
    )(table, h, *ranked, up, *after)


def store_body(first, *refs):
    h_ref, (out_ref, wide_ref, semaphores) = refs[0], refs[-3:]
    rows = h_ref.shape[0]
    extent = rows // PIECES
    copies = []
    for piece in range(PIECES):
        part = pl.ds(piece * extent, extent)
        wide_ref[part, :] = h_ref[part, :].astype(wide_ref.dtype)
        copy = pltpu.make_async_copy(
            wide_ref.at[part], out_ref.at[0, pl.ds(first + piece * extent, extent)], semaphores.at[piece]
        )
        copy.start()
        copies.append(copy)
    for copy in copies:
        copy.wait()


def store(h, first, shape, dtype, out):
    held = [] if out is None else [out]
    return pl.pallas_call(
        functools.partial(store_body, first),
        in_specs=[IN_VMEM] + [ANYWHERE] * len(held),
        out_specs=ANYWHERE,
        out_shape=jax.ShapeDtypeStruct(shape, dtype),
        input_output_aliases={1: 0} if held else {},
        scratch_shapes=[pltpu.VMEM(h.shape, dtype), pltpu.SemaphoreType.DMA((PIECES,))],
        compiler_params=params(),
        cost_estimate=pl.CostEstimate(flops=0, transcendentals=0, bytes_accessed=6 * h.size),
        name="store",
    )(h, *held)


def per_device(stream, down_factor, router, expert_factor, core_tensor, up_factor):
    section_id = lax.axis_index("section")
    sections = lax.axis_size("section")
    parts = lax.axis_size("tensor")
    front_edge = sections // 2
    ticks = jnp.arange(TICKS + 1, dtype=jnp.int32)
    laps = ((section_id - ticks) % sections < front_edge).astype(jnp.int32) + (section_id < ticks).astype(jnp.int32)
    table = jnp.where(ticks < TICKS, laps, lax.axis_index("tensor"))
    expert = jnp.swapaxes(expert_factor[:, 0], 1, 2)
    width = stream.shape[2] * parts
    stream, *stacked = [
        pltpu.with_memory_space_constraint(value, pltpu.HBM)
        for value in (stream, down_factor, router, core_tensor, up_factor)
    ]
    blocks, start = [], 0
    for share in SHARES:
        rows = stream.shape[1] * share // sum(SHARES)
        blocks.append((start, rows))
        start += rows
    *early, front = fetch(table, 0, stream, blocks[:1], stacked[:2], [])
    *late, back = fetch(table, 0, stream, blocks[1:2], stacked[2:], [])
    held = [front, back]

    def exchange(own, square, sent):
        if parts == 2:
            return own, square, [from_behind(sent, "tensor", 1)]
        if parts > 2:
            return lax.psum(own, "tensor"), lax.psum(square, "tensor"), []
        return own, square, []

    def gather(piece):
        if parts > 2:
            return [lax.all_gather(piece, "tensor", axis=1, tiled=True)]
        return [piece] + [from_behind(piece, "tensor", 1)] * (parts - 1)

    steps = TICKS * CHUNKS
    projected = [exchange(*project(held[at], *early, [])) for at in range(LEAD)]
    piece = core(table, 0, *projected[0], expert, late[0], width, [])
    held += fetch(table, 0, stream, blocks[2:], [], [piece])
    for step in range(steps):
        tick, chunk = divmod(step, CHUNKS)
        order = []
        if step + LEAD < steps:
            ahead_tick, ahead = divmod(step + LEAD, CHUNKS)
            own, square, sent = project(held[ahead], *early, [piece])
            order = [sent]
            if ahead == CHUNKS - 1 and ahead_tick + 1 < TICKS:
                early = refresh(table, ahead_tick + 1, stacked[:2], early, order)
                order = order + [early[0]]
            projected.append(exchange(own, square, sent))
        pieces = gather(piece)
        value = advance(table, held[chunk], pieces, late[1], order)
        held[chunk] = from_behind(value, "section", 1)
        if step + 1 < steps:
            if chunk == CHUNKS - 1:
                late = refresh(table, tick + 1, stacked[2:], late, [value])
            piece = core(
                table, (step + 1) // CHUNKS, *projected[step + 1], expert, late[0], width, [value]
            )
    out = None
    for h, (first, _) in zip(held, blocks):
        out = store(h, first, stream.shape, stream.dtype, out)
    return out


def solution(mesh):
    return jax.shard_map(
        per_device,
        mesh=mesh,
        in_specs=(
            P("section", None, "tensor"),
            P(None, "section", "tensor", None),
            P(None, "section", "tensor", None),
            P(None, "section", None, None),
            P(None, "section", "tensor", None, None),
            P(None, "section", None, "tensor"),
        ),
        out_specs=P("section", None, "tensor"),
        check_vma=False,
    )
```

```python
import functools

import jax
import jax.numpy as jnp
from jax import lax
from jax.experimental import pallas as pl
from jax.experimental.pallas import tpu as pltpu
from jax.sharding import PartitionSpec as P


TICKS = 6
SHARES = (4, 4, 4, 4)
CHUNKS = len(SHARES)
LEAD = 2
PIECES = 4
EPSILON = 1e-05
LANES = 128

IN_VMEM = pl.BlockSpec(memory_space=pltpu.VMEM)
IN_HBM = pl.BlockSpec(memory_space=pltpu.HBM)
IN_SMEM = pl.BlockSpec(memory_space=pltpu.SMEM)
ANYWHERE = pl.BlockSpec(memory_space=pl.ANY)


def from_behind(value, axis, steps):
    count = lax.axis_size(axis)
    pairs = [(source, (source + steps) % count) for source in range(count)]
    return lax.ppermute(value, axis, pairs)


def largest_divisor(extent, limit):
    size = min(extent, limit)
    while extent % size:
        size -= 1
    return size


def params():
    return pltpu.CompilerParams(vmem_limit_bytes=10 << 20)


def fetch_copies(sources, targets, semaphores, places):
    copies = []
    for at, (source, target, place) in enumerate(zip(sources, targets, places)):
        extent = target.shape[0] // PIECES
        for piece in range(PIECES):
            copies.append(
                pltpu.make_async_copy(
                    source.at[(*place[:-1], pl.ds(place[-1] + piece * extent, extent))],
                    target.at[pl.ds(piece * extent, extent)],
                    semaphores.at[at, piece],
                )
            )
    return copies


def fetch_body(count, tick, blocks, table_ref, stream_ref, *refs):
    sources, targets, semaphores = refs[:count], refs[-1 - count - len(blocks) : -1], refs[-1]
    lap = table_ref[tick]
    copies = fetch_copies(
        (*sources, *([stream_ref] * len(blocks))),
        targets,
        semaphores,
        [(lap, 0, 0)] * count + [(0, first) for first, _ in blocks],
    )
    for copy in copies:
        copy.start()
    for copy in copies:
        copy.wait()


def fetch(table, tick, stream, blocks, stacked, after):
    count = len(stacked)
    features = stream.shape[2]
    return pl.pallas_call(
        functools.partial(fetch_body, count, tick, blocks),
        in_specs=[IN_SMEM] + [IN_HBM] * (1 + count) + [ANYWHERE] * len(after),
        out_specs=[IN_VMEM] * (count + len(blocks)),
        out_shape=[pltpu.VMEM(value.shape[2:], value.dtype) for value in stacked]
        + [pltpu.VMEM((rows, features), stream.dtype) for _, rows in blocks],
        scratch_shapes=[pltpu.SemaphoreType.DMA((count + len(blocks), PIECES))],
        compiler_params=params(),
        cost_estimate=pl.CostEstimate(
            flops=0, transcendentals=0, bytes_accessed=sum(value.size * value.dtype.itemsize for value in stacked)
        ),
        name="fetch",
    )(table, stream, *stacked, *after)


def refresh_body(count, tick, table_ref, *refs):
    sources = refs[:count]
    targets, semaphores = refs[-1 - count : -1], refs[-1]

    @pl.when(table_ref[tick] != table_ref[tick - 1])
    def _():
        copies = fetch_copies(sources, targets, semaphores, [(table_ref[tick], 0, 0)] * count)
        for copy in copies:
            copy.start()
        for copy in copies:
            copy.wait()


def refresh(table, tick, stacked, resident, after):
    count = len(stacked)
    return pl.pallas_call(
        functools.partial(refresh_body, count, tick),
        in_specs=[IN_SMEM] + [IN_HBM] * count + [IN_VMEM] * count + [ANYWHERE] * len(after),
        out_specs=[IN_VMEM] * count,
        out_shape=[pltpu.VMEM(value.shape, value.dtype) for value in resident],
        input_output_aliases={1 + count + at: at for at in range(count)},
        scratch_shapes=[pltpu.SemaphoreType.DMA((count, PIECES))],
        compiler_params=params(),
        cost_estimate=pl.CostEstimate(flops=0, transcendentals=0, bytes_accessed=0),
        name="refresh",
    )(table, *stacked, *resident, *after)


def open_body(table_ref, stream_ref, down_src, router_src, *rest):
    down_ref, router_ref, h_ref, own_ref, square_ref, sent_ref, semaphores = rest
    rows, features = h_ref.shape
    lap = table_ref[0]
    extent = features // PIECES
    copies = []
    for piece in range(PIECES):
        part = pl.ds(piece * extent, extent)
        copies.append(
            (
                pltpu.make_async_copy(
                    stream_ref.at[0, pl.ds(0, rows), part], h_ref.at[:, part], semaphores.at[0, piece]
                ),
                pltpu.make_async_copy(down_src.at[lap, 0, part], down_ref.at[part], semaphores.at[1, piece]),
                pltpu.make_async_copy(router_src.at[lap, 0, part], router_ref.at[part], semaphores.at[2, piece]),
            )
        )
    for group in copies:
        for copy in group:
            copy.start()
    partial = jnp.zeros((rows, LANES), jnp.float32)
    for piece, group in enumerate(copies):
        for copy in group:
            copy.wait()
        span = slice(piece * extent, (piece + 1) * extent)
        for at in range(span.start, span.stop, LANES):
            wide = h_ref[:, at : at + LANES]
            partial = partial + wide * wide
        low = h_ref[:, span].astype(jnp.bfloat16)
        start = 0
        for weight_ref in (down_ref, router_ref):
            columns = weight_ref.shape[1]
            value = jnp.dot(low, weight_ref[span, :], preferred_element_type=jnp.float32)
            if piece:
                value = value + own_ref[:, start : start + columns]
            own_ref[:, start : start + columns] = value
            if piece == PIECES - 1:
                sent_ref[:, start : start + columns] = value.astype(jnp.bfloat16)
            start += columns
    square = jnp.broadcast_to(jnp.sum(partial, axis=1, keepdims=True), (rows, LANES))
    square_ref[...] = square
    upper = square.astype(jnp.bfloat16).astype(jnp.float32)
    lane = lax.broadcasted_iota(jnp.int32, (rows, LANES), 1)
    sent_ref[:, start:] = jnp.where(lane < LANES // 2, upper, square - upper).astype(jnp.bfloat16)


def open_up(table, stream, rows, stacked):
    features = stream.shape[2]
    total = sum(value.shape[3] for value in stacked)
    return pl.pallas_call(
        open_body,
        in_specs=[IN_SMEM] + [IN_HBM] * 3,
        out_specs=[IN_VMEM] * 6,
        out_shape=[pltpu.VMEM(value.shape[2:], value.dtype) for value in stacked]
        + [
            pltpu.VMEM((rows, features), stream.dtype),
            jax.ShapeDtypeStruct((rows, total), jnp.float32),
            jax.ShapeDtypeStruct((rows, LANES), jnp.float32),
            jax.ShapeDtypeStruct((rows, total + LANES), jnp.bfloat16),
        ],
        scratch_shapes=[pltpu.SemaphoreType.DMA((3, PIECES))],
        compiler_params=params(),
        cost_estimate=pl.CostEstimate(
            flops=2 * rows * features * total, bytes_accessed=2 * features * total, transcendentals=0
        ),
        name="open_up",
    )(table, stream, *stacked)


def project_body(h_ref, down_ref, router_ref, *rest):
    own_ref, square_ref, sent_ref = rest[-3:]
    rows, features = h_ref.shape
    partial = jnp.zeros((rows, LANES), jnp.float32)
    for at in range(0, features, LANES):
        wide = h_ref[:, at : at + LANES].astype(jnp.float32)
        partial = partial + wide * wide
    square = jnp.broadcast_to(jnp.sum(partial, axis=1, keepdims=True), (rows, LANES))
    square_ref[...] = square
    upper = square.astype(jnp.bfloat16)
    lower = (square - upper.astype(jnp.float32)).astype(jnp.bfloat16)
    lane = lax.broadcasted_iota(jnp.int32, (rows, LANES), 1)
    start = 0
    for weight_ref in (down_ref, router_ref):
        extent = weight_ref.shape[1]
        block = largest_divisor(extent, 256)
        for at in range(0, extent, block):
            value = jnp.dot(
                h_ref[...].astype(jnp.bfloat16), weight_ref[:, at : at + block], preferred_element_type=jnp.float32
            )
            own_ref[:, start + at : start + at + block] = value
            sent_ref[:, start + at : start + at + block] = value.astype(jnp.bfloat16)
        start += extent
    sent_ref[:, start:] = jnp.where(
        lane < LANES // 2, upper.astype(jnp.float32), lower.astype(jnp.float32)
    ).astype(jnp.bfloat16)


def project(h, down, router, after):
    rows, features = h.shape
    total = down.shape[1] + router.shape[1]
    return pl.pallas_call(
        project_body,
        in_specs=[IN_VMEM] * 3 + [ANYWHERE] * len(after),
        out_specs=[IN_VMEM] * 3,
        out_shape=[
            jax.ShapeDtypeStruct((rows, total), jnp.float32),
            jax.ShapeDtypeStruct((rows, LANES), jnp.float32),
            jax.ShapeDtypeStruct((rows, total + LANES), jnp.bfloat16),
        ],
        compiler_params=params(),
        cost_estimate=pl.CostEstimate(
            flops=2 * rows * features * total, bytes_accessed=6 * rows * total, transcendentals=0
        ),
        name="project",
    )(h, down, router, *after)


def core_body(others, width, tick, table_ref, own_ref, square_ref, *rest):
    sent_refs = rest[:others]
    expert_ref, core_ref = rest[others : others + 2]
    out_ref, reduced_ref, mixing_ref, ranked_ref = rest[-4:]
    d_rank, rows = reduced_ref.shape
    experts = expert_ref.shape[2]
    lap = table_ref[tick]
    square = square_ref[...]
    tail = d_rank + experts
    for other in sent_refs:
        pair = other[:, tail:].astype(jnp.float32)
        square = square + pair[:, :1] + pair[:, LANES // 2 : LANES // 2 + 1]
    factor = lax.rsqrt(square / width + EPSILON)

    def total(at):
        value = own_ref[:, at : at + LANES]
        for other in sent_refs:
            value = value + other[:, at : at + LANES].astype(jnp.float32)
        return value

    for at in range(0, d_rank, LANES):
        reduced_ref[at : at + LANES, :] = (total(at) * factor).astype(jnp.bfloat16).T
    mixing = jnp.zeros(mixing_ref.shape, jnp.float32)
    for at in range(0, experts, LANES):
        gating = jax.nn.sigmoid(total(d_rank + at) * factor).astype(jnp.bfloat16)
        mixing = mixing + lax.dot_general(
            expert_ref[lap, :, at : at + LANES],
            gating,
            (((1,), (1,)), ((), ())),
            preferred_element_type=jnp.float32,
        )
    mixing_ref[...] = mixing.astype(jnp.bfloat16).astype(jnp.float32)

    f_rank, ranks, depth = core_ref.shape
    group = largest_divisor(f_rank, 32)
    for at in range(0, f_rank, group):
        part = core_ref[at : at + group].reshape(group * ranks, depth)
        value = jnp.dot(part, reduced_ref[...], preferred_element_type=jnp.float32)
        value = value.reshape(group, ranks, rows) * mixing_ref[...][None]
        ranked_ref[at : at + group, :] = jnp.sum(value, axis=1)
    out_ref[...] = ranked_ref[...].T.astype(jnp.bfloat16)


def core(table, tick, own, square, sent, expert, core_tensor, width, after):
    rows = own.shape[0]
    f_rank, ranks, d_rank = core_tensor.shape
    others = len(sent)
    return pl.pallas_call(
        functools.partial(core_body, others, width, tick),
        in_specs=[IN_SMEM] + [IN_VMEM] * (4 + others) + [ANYWHERE] * len(after),
        out_specs=IN_VMEM,
        out_shape=jax.ShapeDtypeStruct((rows, f_rank), jnp.bfloat16),
        scratch_shapes=[
            pltpu.VMEM((d_rank, rows), jnp.bfloat16),
            pltpu.VMEM((ranks, rows), jnp.float32),
            pltpu.VMEM((f_rank, rows), jnp.float32),
        ],
        compiler_params=params(),
        cost_estimate=pl.CostEstimate(
            flops=2 * rows * f_rank * ranks * d_rank, bytes_accessed=6 * rows * d_rank, transcendentals=rows * d_rank
        ),
        name="core",
    )(table, own, square, *sent, expert, core_tensor, *after)


def advance_body(pieces, table_ref, h_ref, *rest):
    ranked, up_ref, out_ref = rest[:pieces], rest[pieces], rest[-1]
    features = h_ref.shape[1]
    extent = ranked[0].shape[1]
    block = largest_divisor(features, 512)
    for at in range(0, features, block):
        value = h_ref[:, at : at + block].astype(jnp.float32)
        for shift, piece in enumerate(ranked):
            row = pl.multiple_of(lax.rem(table_ref[TICKS] + pieces - shift, pieces) * extent, extent)
            value = value + jnp.dot(
                piece[...], up_ref[pl.ds(row, extent), at : at + block], preferred_element_type=jnp.float32
            )
        out_ref[:, at : at + block] = value.astype(jnp.bfloat16)


def advance(table, h, ranked, up, after):
    pieces = len(ranked)
    rows, features = h.shape
    return pl.pallas_call(
        functools.partial(advance_body, pieces),
        in_specs=[IN_SMEM] + [IN_VMEM] * (2 + pieces) + [ANYWHERE] * len(after),
        out_specs=IN_VMEM,
        out_shape=jax.ShapeDtypeStruct((rows, features), jnp.bfloat16),
        compiler_params=params(),
        cost_estimate=pl.CostEstimate(
            flops=2 * rows * up.shape[0] * features, bytes_accessed=4 * rows * features, transcendentals=0
        ),
        name="advance",
    )(table, h, *ranked, up, *after)


def store_body(first, *refs):
    h_ref, (out_ref, wide_ref, semaphores) = refs[0], refs[-3:]
    rows = h_ref.shape[0]
    extent = rows // PIECES
    copies = []
    for piece in range(PIECES):
        part = pl.ds(piece * extent, extent)
        wide_ref[part, :] = h_ref[part, :].astype(wide_ref.dtype)
        copy = pltpu.make_async_copy(
            wide_ref.at[part], out_ref.at[0, pl.ds(first + piece * extent, extent)], semaphores.at[piece]
        )
        copy.start()
        copies.append(copy)
    for copy in copies:
        copy.wait()


def store(h, first, shape, dtype, out):
    held = [] if out is None else [out]
    return pl.pallas_call(
        functools.partial(store_body, first),
        in_specs=[IN_VMEM] + [ANYWHERE] * len(held),
        out_specs=ANYWHERE,
        out_shape=jax.ShapeDtypeStruct(shape, dtype),
        input_output_aliases={1: 0} if held else {},
        scratch_shapes=[pltpu.VMEM(h.shape, dtype), pltpu.SemaphoreType.DMA((PIECES,))],
        compiler_params=params(),
        cost_estimate=pl.CostEstimate(flops=0, transcendentals=0, bytes_accessed=6 * h.size),
        name="store",
    )(h, *held)


def per_device(stream, down_factor, router, expert_factor, core_tensor, up_factor):
    section_id = lax.axis_index("section")
    sections = lax.axis_size("section")
    parts = lax.axis_size("tensor")
    front_edge = sections // 2
    ticks = jnp.arange(TICKS + 1, dtype=jnp.int32)
    laps = ((section_id - ticks) % sections < front_edge).astype(jnp.int32) + (section_id < ticks).astype(jnp.int32)
    table = jnp.where(ticks < TICKS, laps, lax.axis_index("tensor"))
    expert = jnp.swapaxes(expert_factor[:, 0], 1, 2)
    width = stream.shape[2] * parts
    stream, *stacked = [
        pltpu.with_memory_space_constraint(value, pltpu.HBM)
        for value in (stream, down_factor, router, core_tensor, up_factor)
    ]
    blocks, start = [], 0
    for share in SHARES:
        rows = stream.shape[1] * share // sum(SHARES)
        blocks.append((start, rows))
        start += rows
    *early, front, own, square, sent = open_up(table, stream, blocks[0][1], stacked[:2])
    *late, back = fetch(table, 0, stream, blocks[1:2], stacked[2:], [])
    held = [front, back]

    def exchange(own, square, sent):
        if parts == 2:
            return own, square, [from_behind(sent, "tensor", 1)]
        if parts > 2:
            return lax.psum(own, "tensor"), lax.psum(square, "tensor"), []
        return own, square, []

    def gather(piece):
        if parts > 2:
            return [lax.all_gather(piece, "tensor", axis=1, tiled=True)]
        return [piece] + [from_behind(piece, "tensor", 1)] * (parts - 1)

    steps = TICKS * CHUNKS
    projected = [exchange(own, square, sent)]
    projected += [exchange(*project(held[at], *early, [])) for at in range(1, LEAD)]
    piece = core(table, 0, *projected[0], expert, late[0], width, [])
    held += fetch(table, 0, stream, blocks[2:], [], [piece])
    for step in range(steps):
        tick, chunk = divmod(step, CHUNKS)
        order = []
        if step + LEAD < steps:
            ahead_tick, ahead = divmod(step + LEAD, CHUNKS)
            own, square, sent = project(held[ahead], *early, [piece])
            order = [sent]
            if ahead == CHUNKS - 1 and ahead_tick + 1 < TICKS:
                early = refresh(table, ahead_tick + 1, stacked[:2], early, order)
                order = order + [early[0]]
            projected.append(exchange(own, square, sent))
        pieces = gather(piece)
        value = advance(table, held[chunk], pieces, late[1], order)
        held[chunk] = from_behind(value, "section", 1)
        if step + 1 < steps:
            if chunk == CHUNKS - 1:
                late = refresh(table, tick + 1, stacked[2:], late, [value])
            piece = core(
                table, (step + 1) // CHUNKS, *projected[step + 1], expert, late[0], width, [value]
            )
    out = None
    for h, (first, _) in zip(held, blocks):
        out = store(h, first, stream.shape, stream.dtype, out)
    return out


def solution(mesh):
    return jax.shard_map(
        per_device,
        mesh=mesh,
        in_specs=(
            P("section", None, "tensor"),
            P(None, "section", "tensor", None),
            P(None, "section", "tensor", None),
            P(None, "section", None, None),
            P(None, "section", "tensor", None, None),
            P(None, "section", None, "tensor"),
        ),
        out_specs=P("section", None, "tensor"),
        check_vma=False,
    )
```

```python
import functools

import jax
import jax.numpy as jnp
from jax import lax
from jax.experimental import pallas as pl
from jax.experimental.pallas import tpu as pltpu
from jax.sharding import PartitionSpec as P


TICKS = 6
SHARES = (4, 4, 4, 4)
CHUNKS = len(SHARES)
LEAD = 2
PIECES = 4
EPSILON = 1e-05
LANES = 128

IN_VMEM = pl.BlockSpec(memory_space=pltpu.VMEM)
IN_HBM = pl.BlockSpec(memory_space=pltpu.HBM)
IN_SMEM = pl.BlockSpec(memory_space=pltpu.SMEM)
ANYWHERE = pl.BlockSpec(memory_space=pl.ANY)


def from_behind(value, axis, steps):
    count = lax.axis_size(axis)
    pairs = [(source, (source + steps) % count) for source in range(count)]
    return lax.ppermute(value, axis, pairs)


def largest_divisor(extent, limit):
    size = min(extent, limit)
    while extent % size:
        size -= 1
    return size


def params():
    return pltpu.CompilerParams(vmem_limit_bytes=10 << 20)


def fetch_copies(sources, targets, semaphores, places):
    copies = []
    for at, (source, target, place) in enumerate(zip(sources, targets, places)):
        extent = target.shape[0] // PIECES
        for piece in range(PIECES):
            copies.append(
                pltpu.make_async_copy(
                    source.at[(*place[:-1], pl.ds(place[-1] + piece * extent, extent))],
                    target.at[pl.ds(piece * extent, extent)],
                    semaphores.at[at, piece],
                )
            )
    return copies


def fetch_body(count, tick, blocks, table_ref, stream_ref, *refs):
    sources, targets, semaphores = refs[:count], refs[-1 - count - len(blocks) : -1], refs[-1]
    lap = table_ref[tick]
    copies = fetch_copies(
        (*sources, *([stream_ref] * len(blocks))),
        targets,
        semaphores,
        [(lap, 0, 0)] * count + [(0, first) for first, _ in blocks],
    )
    for copy in copies:
        copy.start()
    for copy in copies:
        copy.wait()


def fetch(table, tick, stream, blocks, stacked, after):
    count = len(stacked)
    features = stream.shape[2]
    return pl.pallas_call(
        functools.partial(fetch_body, count, tick, blocks),
        in_specs=[IN_SMEM] + [IN_HBM] * (1 + count) + [ANYWHERE] * len(after),
        out_specs=[IN_VMEM] * (count + len(blocks)),
        out_shape=[pltpu.VMEM(value.shape[2:], value.dtype) for value in stacked]
        + [pltpu.VMEM((rows, features), stream.dtype) for _, rows in blocks],
        scratch_shapes=[pltpu.SemaphoreType.DMA((count + len(blocks), PIECES))],
        compiler_params=params(),
        cost_estimate=pl.CostEstimate(
            flops=0, transcendentals=0, bytes_accessed=sum(value.size * value.dtype.itemsize for value in stacked)
        ),
        name="fetch",
    )(table, stream, *stacked, *after)


def refresh_body(count, tick, table_ref, *refs):
    sources = refs[:count]
    targets, semaphores = refs[-1 - count : -1], refs[-1]

    @pl.when(table_ref[tick] != table_ref[tick - 1])
    def _():
        copies = fetch_copies(sources, targets, semaphores, [(table_ref[tick], 0, 0)] * count)
        for copy in copies:
            copy.start()
        for copy in copies:
            copy.wait()


def refresh(table, tick, stacked, resident, after):
    count = len(stacked)
    return pl.pallas_call(
        functools.partial(refresh_body, count, tick),
        in_specs=[IN_SMEM] + [IN_HBM] * count + [IN_VMEM] * count + [ANYWHERE] * len(after),
        out_specs=[IN_VMEM] * count,
        out_shape=[pltpu.VMEM(value.shape, value.dtype) for value in resident],
        input_output_aliases={1 + count + at: at for at in range(count)},
        scratch_shapes=[pltpu.SemaphoreType.DMA((count, PIECES))],
        compiler_params=params(),
        cost_estimate=pl.CostEstimate(flops=0, transcendentals=0, bytes_accessed=0),
        name="refresh",
    )(table, *stacked, *resident, *after)


def open_body(table_ref, stream_ref, down_src, router_src, *rest):
    down_ref, router_ref, h_ref, own_ref, square_ref, sent_ref, semaphores = rest
    rows, features = h_ref.shape
    lap = table_ref[0]
    pieces = semaphores.shape[1]
    extent = features // pieces
    copies = []
    for piece in range(pieces):
        part = pl.ds(piece * extent, extent)
        copies.append(
            (
                pltpu.make_async_copy(
                    stream_ref.at[0, pl.ds(0, rows), part], h_ref.at[:, part], semaphores.at[0, piece]
                ),
                pltpu.make_async_copy(down_src.at[lap, 0, part], down_ref.at[part], semaphores.at[1, piece]),
                pltpu.make_async_copy(router_src.at[lap, 0, part], router_ref.at[part], semaphores.at[2, piece]),
            )
        )
    for group in copies:
        for copy in group:
            copy.start()
    partial = jnp.zeros((rows, LANES), jnp.float32)
    for piece, group in enumerate(copies):
        for copy in group:
            copy.wait()
        span = slice(piece * extent, (piece + 1) * extent)
        for at in range(span.start, span.stop, LANES):
            wide = h_ref[:, at : at + LANES]
            partial = partial + wide * wide
        low = h_ref[:, span].astype(jnp.bfloat16)
        start = 0
        for weight_ref in (down_ref, router_ref):
            columns = weight_ref.shape[1]
            value = jnp.dot(low, weight_ref[span, :], preferred_element_type=jnp.float32)
            if piece:
                value = value + own_ref[:, start : start + columns]
            own_ref[:, start : start + columns] = value
            if piece == pieces - 1:
                sent_ref[:, start : start + columns] = value.astype(jnp.bfloat16)
            start += columns
    square = jnp.broadcast_to(jnp.sum(partial, axis=1, keepdims=True), (rows, LANES))
    square_ref[...] = square
    upper = square.astype(jnp.bfloat16).astype(jnp.float32)
    lane = lax.broadcasted_iota(jnp.int32, (rows, LANES), 1)
    sent_ref[:, start:] = jnp.where(lane < LANES // 2, upper, square - upper).astype(jnp.bfloat16)


def open_up(table, stream, rows, stacked):
    features = stream.shape[2]
    total = sum(value.shape[3] for value in stacked)
    return pl.pallas_call(
        open_body,
        in_specs=[IN_SMEM] + [IN_HBM] * 3,
        out_specs=[IN_VMEM] * 6,
        out_shape=[pltpu.VMEM(value.shape[2:], value.dtype) for value in stacked]
        + [
            pltpu.VMEM((rows, features), stream.dtype),
            jax.ShapeDtypeStruct((rows, total), jnp.float32),
            jax.ShapeDtypeStruct((rows, LANES), jnp.float32),
            jax.ShapeDtypeStruct((rows, total + LANES), jnp.bfloat16),
        ],
        scratch_shapes=[pltpu.SemaphoreType.DMA((3, min(2 * PIECES, features // LANES)))],
        compiler_params=params(),
        cost_estimate=pl.CostEstimate(
            flops=2 * rows * features * total, bytes_accessed=2 * features * total, transcendentals=0
        ),
        name="open_up",
    )(table, stream, *stacked)


def project_body(h_ref, down_ref, router_ref, *rest):
    own_ref, square_ref, sent_ref = rest[-3:]
    rows, features = h_ref.shape
    partial = jnp.zeros((rows, LANES), jnp.float32)
    for at in range(0, features, LANES):
        wide = h_ref[:, at : at + LANES].astype(jnp.float32)
        partial = partial + wide * wide
    square = jnp.broadcast_to(jnp.sum(partial, axis=1, keepdims=True), (rows, LANES))
    square_ref[...] = square
    upper = square.astype(jnp.bfloat16)
    lower = (square - upper.astype(jnp.float32)).astype(jnp.bfloat16)
    lane = lax.broadcasted_iota(jnp.int32, (rows, LANES), 1)
    start = 0
    for weight_ref in (down_ref, router_ref):
        extent = weight_ref.shape[1]
        block = largest_divisor(extent, 256)
        for at in range(0, extent, block):
            value = jnp.dot(
                h_ref[...].astype(jnp.bfloat16), weight_ref[:, at : at + block], preferred_element_type=jnp.float32
            )
            own_ref[:, start + at : start + at + block] = value
            sent_ref[:, start + at : start + at + block] = value.astype(jnp.bfloat16)
        start += extent
    sent_ref[:, start:] = jnp.where(
        lane < LANES // 2, upper.astype(jnp.float32), lower.astype(jnp.float32)
    ).astype(jnp.bfloat16)


def project(h, down, router, after):
    rows, features = h.shape
    total = down.shape[1] + router.shape[1]
    return pl.pallas_call(
        project_body,
        in_specs=[IN_VMEM] * 3 + [ANYWHERE] * len(after),
        out_specs=[IN_VMEM] * 3,
        out_shape=[
            jax.ShapeDtypeStruct((rows, total), jnp.float32),
            jax.ShapeDtypeStruct((rows, LANES), jnp.float32),
            jax.ShapeDtypeStruct((rows, total + LANES), jnp.bfloat16),
        ],
        compiler_params=params(),
        cost_estimate=pl.CostEstimate(
            flops=2 * rows * features * total, bytes_accessed=6 * rows * total, transcendentals=0
        ),
        name="project",
    )(h, down, router, *after)


def core_body(others, width, tick, table_ref, own_ref, square_ref, *rest):
    sent_refs = rest[:others]
    expert_ref, core_ref = rest[others : others + 2]
    out_ref, reduced_ref, mixing_ref, ranked_ref = rest[-4:]
    d_rank, rows = reduced_ref.shape
    experts = expert_ref.shape[2]
    lap = table_ref[tick]
    square = square_ref[...]
    tail = d_rank + experts
    for other in sent_refs:
        pair = other[:, tail:].astype(jnp.float32)
        square = square + pair[:, :1] + pair[:, LANES // 2 : LANES // 2 + 1]
    factor = lax.rsqrt(square / width + EPSILON)

    def total(at):
        value = own_ref[:, at : at + LANES]
        for other in sent_refs:
            value = value + other[:, at : at + LANES].astype(jnp.float32)
        return value

    for at in range(0, d_rank, LANES):
        reduced_ref[at : at + LANES, :] = (total(at) * factor).astype(jnp.bfloat16).T
    mixing = jnp.zeros(mixing_ref.shape, jnp.float32)
    for at in range(0, experts, LANES):
        gating = jax.nn.sigmoid(total(d_rank + at) * factor).astype(jnp.bfloat16)
        mixing = mixing + lax.dot_general(
            expert_ref[lap, :, at : at + LANES],
            gating,
            (((1,), (1,)), ((), ())),
            preferred_element_type=jnp.float32,
        )
    mixing_ref[...] = mixing.astype(jnp.bfloat16).astype(jnp.float32)

    f_rank, ranks, depth = core_ref.shape
    group = largest_divisor(f_rank, 32)
    for at in range(0, f_rank, group):
        part = core_ref[at : at + group].reshape(group * ranks, depth)
        value = jnp.dot(part, reduced_ref[...], preferred_element_type=jnp.float32)
        value = value.reshape(group, ranks, rows) * mixing_ref[...][None]
        ranked_ref[at : at + group, :] = jnp.sum(value, axis=1)
    out_ref[...] = ranked_ref[...].T.astype(jnp.bfloat16)


def core(table, tick, own, square, sent, expert, core_tensor, width, after):
    rows = own.shape[0]
    f_rank, ranks, d_rank = core_tensor.shape
    others = len(sent)
    return pl.pallas_call(
        functools.partial(core_body, others, width, tick),
        in_specs=[IN_SMEM] + [IN_VMEM] * (4 + others) + [ANYWHERE] * len(after),
        out_specs=IN_VMEM,
        out_shape=jax.ShapeDtypeStruct((rows, f_rank), jnp.bfloat16),
        scratch_shapes=[
            pltpu.VMEM((d_rank, rows), jnp.bfloat16),
            pltpu.VMEM((ranks, rows), jnp.float32),
            pltpu.VMEM((f_rank, rows), jnp.float32),
        ],
        compiler_params=params(),
        cost_estimate=pl.CostEstimate(
            flops=2 * rows * f_rank * ranks * d_rank, bytes_accessed=6 * rows * d_rank, transcendentals=rows * d_rank
        ),
        name="core",
    )(table, own, square, *sent, expert, core_tensor, *after)


def advance_body(pieces, table_ref, h_ref, *rest):
    ranked, up_ref, out_ref = rest[:pieces], rest[pieces], rest[-1]
    features = h_ref.shape[1]
    extent = ranked[0].shape[1]
    block = largest_divisor(features, 512)
    for at in range(0, features, block):
        value = h_ref[:, at : at + block].astype(jnp.float32)
        for shift, piece in enumerate(ranked):
            row = pl.multiple_of(lax.rem(table_ref[TICKS] + pieces - shift, pieces) * extent, extent)
            value = value + jnp.dot(
                piece[...], up_ref[pl.ds(row, extent), at : at + block], preferred_element_type=jnp.float32
            )
        out_ref[:, at : at + block] = value.astype(jnp.bfloat16)


def advance(table, h, ranked, up, after):
    pieces = len(ranked)
    rows, features = h.shape
    return pl.pallas_call(
        functools.partial(advance_body, pieces),
        in_specs=[IN_SMEM] + [IN_VMEM] * (2 + pieces) + [ANYWHERE] * len(after),
        out_specs=IN_VMEM,
        out_shape=jax.ShapeDtypeStruct((rows, features), jnp.bfloat16),
        compiler_params=params(),
        cost_estimate=pl.CostEstimate(
            flops=2 * rows * up.shape[0] * features, bytes_accessed=4 * rows * features, transcendentals=0
        ),
        name="advance",
    )(table, h, *ranked, up, *after)


def store_body(first, *refs):
    h_ref, (out_ref, wide_ref, semaphores) = refs[0], refs[-3:]
    rows = h_ref.shape[0]
    extent = rows // PIECES
    copies = []
    for piece in range(PIECES):
        part = pl.ds(piece * extent, extent)
        wide_ref[part, :] = h_ref[part, :].astype(wide_ref.dtype)
        copy = pltpu.make_async_copy(
            wide_ref.at[part], out_ref.at[0, pl.ds(first + piece * extent, extent)], semaphores.at[piece]
        )
        copy.start()
        copies.append(copy)
    for copy in copies:
        copy.wait()


def store(h, first, shape, dtype, out):
    held = [] if out is None else [out]
    return pl.pallas_call(
        functools.partial(store_body, first),
        in_specs=[IN_VMEM] + [ANYWHERE] * len(held),
        out_specs=ANYWHERE,
        out_shape=jax.ShapeDtypeStruct(shape, dtype),
        input_output_aliases={1: 0} if held else {},
        scratch_shapes=[pltpu.VMEM(h.shape, dtype), pltpu.SemaphoreType.DMA((PIECES,))],
        compiler_params=params(),
        cost_estimate=pl.CostEstimate(flops=0, transcendentals=0, bytes_accessed=6 * h.size),
        name="store",
    )(h, *held)


def per_device(stream, down_factor, router, expert_factor, core_tensor, up_factor):
    section_id = lax.axis_index("section")
    sections = lax.axis_size("section")
    parts = lax.axis_size("tensor")
    front_edge = sections // 2
    ticks = jnp.arange(TICKS + 1, dtype=jnp.int32)
    laps = ((section_id - ticks) % sections < front_edge).astype(jnp.int32) + (section_id < ticks).astype(jnp.int32)
    table = jnp.where(ticks < TICKS, laps, lax.axis_index("tensor"))
    expert = jnp.swapaxes(expert_factor[:, 0], 1, 2)
    width = stream.shape[2] * parts
    stream, *stacked = [
        pltpu.with_memory_space_constraint(value, pltpu.HBM)
        for value in (stream, down_factor, router, core_tensor, up_factor)
    ]
    blocks, start = [], 0
    for share in SHARES:
        rows = stream.shape[1] * share // sum(SHARES)
        blocks.append((start, rows))
        start += rows
    *early, front, own, square, sent = open_up(table, stream, blocks[0][1], stacked[:2])
    *late, back = fetch(table, 0, stream, blocks[1:2], stacked[2:], [])
    held = [front, back]

    def exchange(own, square, sent):
        if parts == 2:
            return own, square, [from_behind(sent, "tensor", 1)]
        if parts > 2:
            return lax.psum(own, "tensor"), lax.psum(square, "tensor"), []
        return own, square, []

    def gather(piece):
        if parts > 2:
            return [lax.all_gather(piece, "tensor", axis=1, tiled=True)]
        return [piece] + [from_behind(piece, "tensor", 1)] * (parts - 1)

    steps = TICKS * CHUNKS
    projected = [exchange(own, square, sent)]
    projected += [exchange(*project(held[at], *early, [])) for at in range(1, LEAD)]
    piece = core(table, 0, *projected[0], expert, late[0], width, [])
    held += fetch(table, 0, stream, blocks[2:], [], [piece])
    for step in range(steps):
        tick, chunk = divmod(step, CHUNKS)
        order = []
        if step + LEAD < steps:
            ahead_tick, ahead = divmod(step + LEAD, CHUNKS)
            own, square, sent = project(held[ahead], *early, [piece])
            order = [sent]
            if ahead == CHUNKS - 1 and ahead_tick + 1 < TICKS:
                early = refresh(table, ahead_tick + 1, stacked[:2], early, order)
                order = order + [early[0]]
            projected.append(exchange(own, square, sent))
        pieces = gather(piece)
        value = advance(table, held[chunk], pieces, late[1], order)
        held[chunk] = from_behind(value, "section", 1)
        if step + 1 < steps:
            if chunk == CHUNKS - 1:
                late = refresh(table, tick + 1, stacked[2:], late, [value])
            piece = core(
                table, (step + 1) // CHUNKS, *projected[step + 1], expert, late[0], width, [value]
            )
    out = None
    for h, (first, _) in zip(held, blocks):
        out = store(h, first, stream.shape, stream.dtype, out)
    return out


def solution(mesh):
    return jax.shard_map(
        per_device,
        mesh=mesh,
        in_specs=(
            P("section", None, "tensor"),
            P(None, "section", "tensor", None),
            P(None, "section", "tensor", None),
            P(None, "section", None, None),
            P(None, "section", "tensor", None, None),
            P(None, "section", None, "tensor"),
        ),
        out_specs=P("section", None, "tensor"),
        check_vma=False,
    )
```
